256 devices in a mesh: lon: 64 (over y, x_lo, z), lat: 4 (over x_hi, core).
Axes of the slice: x: 4 (x_hi: 2, x_lo: 2; x = x_hi * 2 + x_lo), y: 4, z: 8, core: 2. Of those that a mesh axis runs over, the one named last changes fastest.
Arguments:
- inputs: bfloat16 [32, 4096, 384], P('lat', 'lon'), may hold values from -16 to 16
- conv1_weight: bfloat16 [3, 3, 384, 384], replicated, may hold values from -0.109375 to 0.109375
- conv2_weight: bfloat16 [3, 3, 384, 384], replicated, may hold values from -0.109375 to 0.109375
- cotangent: bfloat16 [32, 4096, 384], P('lat', 'lon'), may hold values from -16 to 16
Outputs:
- output: bfloat16 [32, 4096, 384], P('lat', 'lon')
- input_grad: bfloat16 [32, 4096, 384], P('lat', 'lon')
- conv1_grad: float32 [3, 3, 384, 384], P(None, None, 'lon', 'lat')
- conv2_grad: float32 [3, 3, 384, 384], P(None, None, 'lon', 'lat')
The draws below stay inside these ranges and needn't reach their ends.
All inputs are finite; a program needn't handle non-finite values.
Results may differ from the reference program's by a relative error of at most 0.0033.
Values may be sent and summed in bfloat16 or wider, within the bound.
A program may use at most 128 MiB of HBM per device.

```python
import jax
import jax.numpy as jnp
from jax import lax

C = 384
KERNEL_SPREAD = 64
LAT = 32
LON = 4096


def spiked(drawn, own_key, source, target, shards_of, factor):
    owner, partner = [(jnp.arange(drawn.shape[position]) // (drawn.shape[position] // shards_of)).reshape([-1 if axis == position else 1 for axis in range(drawn.ndim)]) for position in (source, target)]
    chosen = jax.random.permutation(own_key, shards_of)[partner]
    strong = (owner == chosen) | (owner == (partner + shards_of // 2) % shards_of)
    return jnp.where(strong, factor * drawn, drawn)


def block_levels(stream_key, dims, shards, smallest, high):
    gain, own = 1.0, jax.random.fold_in(stream_key, 6)
    for axis_at, parts in shards:
        steps = jnp.exp(jax.random.uniform(jax.random.fold_in(own, axis_at), (parts,), jnp.float32, smallest / len(shards), high / len(shards)))
        gain = gain * jnp.repeat(steps, dims[axis_at] // parts).reshape([-1 if axis == axis_at else 1 for axis in range(len(dims))])
    return gain


def noise(stream_key, dims, scale, limit, cuts=(), dtype=jnp.bfloat16):
    loudness = block_levels(stream_key, dims, cuts, -0.22, 0.18) if cuts else 1.0
    entries = jax.random.normal(stream_key, dims, jnp.float32) * scale * loudness
    return jnp.minimum(jnp.maximum(entries, -limit), limit).astype(dtype)


def noise_with(stream_key, extent, scale, limit, cuts, heavy, kind=jnp.bfloat16):
    result = scale * jax.random.normal(stream_key, extent, jnp.float32)
    if cuts:
        result = result * block_levels(stream_key, extent, cuts, -0.22, 0.18)
    return jnp.clip(spiked(result, jax.random.fold_in(stream_key, 3), *heavy), -limit, limit).astype(kind)


def setup_inputs(seed: int = 0) -> dict:
    key_of = jax.random.split(jax.random.key(seed), 5)
    inputs = noise_with(key_of[0], (LAT, LON, C), 1.0, 16.0, ((0, 4), (1, 64)), (1, 2, 64, 4.0))
    conv1_weight = noise(key_of[1], (3, 3, C, C), (9 * C) ** -0.5, 0.109375)
    conv2_weight = noise(key_of[2], (3, 3, C, C), (9 * C) ** -0.5, 0.109375)
    cotangent = noise_with(key_of[3], (LAT, LON, C), 1.0, 16.0, ((0, 4), (1, 64)), (1, 2, 64, 4.0))
    return dict(inputs=inputs, conv1_weight=conv1_weight, conv2_weight=conv2_weight, cotangent=cotangent)


def shifted(field, lat_step, longitude_stride):
    padded_field = jnp.pad(field, ((1, 1), (0, 0), (0, 0)))
    part = padded_field[1 + lat_step:1 + lat_step + LAT]
    return jnp.roll(part, -KERNEL_SPREAD * longitude_stride, axis=1)

def convolve(field, weight, direction):
    total = jnp.zeros((LAT * LON, C), jnp.float32)
    for lat_step in (-1, 0, 1):
        for longitude_stride in (-1, 0, 1):
            tap = weight[lat_step + 1, longitude_stride + 1].astype(jnp.float32)
            if direction < 0:
                tap = tap.T
            moved = shifted(field, direction * lat_step, direction * longitude_stride).reshape(LAT * LON, C)
            total = total + jnp.dot(moved, tap, precision=lax.Precision.HIGHEST)
    return total

def kernel_grad(field, grad, scale):
    rows = []
    for lat_step in (-1, 0, 1):
        row = []
        for longitude_stride in (-1, 0, 1):
            moved = shifted(field, lat_step, longitude_stride).reshape(LAT * LON, C)
            row.append(jnp.dot(moved.T, grad, precision=lax.Precision.HIGHEST) * scale)
        rows.append(jnp.stack(row))
    return jnp.stack(rows)

def reference(inputs, conv1_weight, conv2_weight, cotangent):
    scale = (LAT * LON) ** (-0.5)
    source = inputs.astype(jnp.float32)
    first = convolve(source, conv1_weight, 1)
    cdf = 0.5 * (1.0 + jax.scipy.special.erf(first / jnp.sqrt(2.0)))
    hidden = (first * cdf).astype(jnp.bfloat16)
    hidden_field = hidden.astype(jnp.float32).reshape(LAT, LON, C)
    second = convolve(hidden_field, conv2_weight, 1)
    output = (source.reshape(LAT * LON, C) + second).astype(jnp.bfloat16).reshape(LAT, LON, C)
    upward = cotangent.astype(jnp.float32)
    upstream = convolve(upward, conv2_weight, -1)
    density = jnp.exp(-0.5 * first * first) / jnp.sqrt(2.0 * jnp.pi)
    pre_grad = (upstream * (cdf + first * density)).astype(jnp.bfloat16)
    pre_field = pre_grad.astype(jnp.float32).reshape(LAT, LON, C)
    back = convolve(pre_field, conv1_weight, -1)
    input_grad = (upward.reshape(LAT * LON, C) + back).astype(jnp.bfloat16).reshape(LAT, LON, C)
    conv2_grad = kernel_grad(hidden_field, upward.reshape(LAT * LON, C), scale)
    conv1_grad = kernel_grad(source, pre_grad.astype(jnp.float32), scale)
    return (output, input_grad, conv1_grad, conv2_grad)
```

```python
import functools

import jax
import jax.numpy as jnp
import numpy as np
from jax import lax
from jax.experimental import pallas as pl
from jax.experimental.pallas import tpu as pltpu
from jax.sharding import PartitionSpec as P

MESH = pl.DeviceIdType.MESH
BF = jnp.bfloat16
F32 = jnp.float32

NY, NX, NZ = 4, 4, 8
NLON, NLAT = 64, 4
R, W, C = 8, 64, 384
TAPS, HALF = 9, 5
YC, XC, ZC = 96, 48, 6


def selection():
    pick = np.zeros((NZ * 32, HALF * XC), np.float32)
    for z in range(NZ):
        for t in range(HALF):
            for r in range(ZC):
                pick[z * 32 + t * ZC + r, t * XC + z * ZC + r] = 1.0
    return pick


def kernel(
    x_hbm, c_hbm, w1_hbm, w2_hbm, pick_ref,
    out_hbm, ig_hbm, g_hbm,
    fld, w1, w2, wt1, wt2, acc, dg, obuf, oth, oth2, ft, term,
    r1a, r1b, s1a, s1b, r2, u, zs, r3, po, go,
    ssem, rsem, osem, orem, o2s, o2r, r1s, r1r, r2s, r2r, r3s, r3r, r4s, r4r, lsem,
    *, scale,
):
    lon, lat = lax.axis_index("lon"), lax.axis_index("lat")
    y, xl, z = lon // 16, (lon // 8) % 2, lon % 8
    xh, core = lat // 2, lat % 2
    x = xh * 2 + xl
    east, west = (lon + 1) % NLON, (lon + NLON - 1) % NLON
    sib = xh * 2 + 1 - core

    def dev(o, a):
        return {"lon": o, "lat": a}

    def at_y(k):
        return dev((((y + k) % NY) * 2 + xl) * NZ + z, lat), (y + k) % NY

    def at_x(k):
        xx = (x + k) % NX
        return dev((y * 2 + xx % 2) * NZ + z, (xx // 2) * 2 + core), xx // 2, xx % 2

    def at_z(k):
        zz = (z + k) % NZ
        return dev((y * 2 + xl) * NZ + zz, lat), zz

    hbm = (x_hbm, c_hbm)
    own = [pltpu.make_async_copy(hbm[f], fld.at[f, 1, pl.ds(1, R)], lsem.at[f]) for f in range(2)]
    wload = [pltpu.make_async_copy(s, d, lsem.at[2 + i]) for i, (s, d) in enumerate(((w1_hbm, w1), (w2_hbm, w2)))]
    for cp in own + wload:
        cp.start()

    barrier = pltpu.get_barrier_semaphore()
    peers = [dev(east, lat), dev(west, lat)] + [dev(lon, (lat + k) % NLAT) for k in (1, 2, 3)]
    peers += [at_y(k)[0] for k in (1, 2, 3)] + [at_x(k)[0] for k in (1, 2, 3)] + [at_z(k)[0] for k in range(1, NZ)]
    for peer in peers:
        pl.semaphore_signal(barrier, inc=1, device_id=peer, device_id_type=MESH)
    pl.semaphore_wait(barrier, len(peers))

    def remote(src, dst, s, r, device):
        return pltpu.make_async_remote_copy(
            src_ref=src, dst_ref=dst, send_sem=s, recv_sem=r, device_id=device, device_id_type=MESH
        )

    parts = ((0, 1), (R - 1, 1), (1, R - 2))

    def ew(f, d, p):
        at, n = parts[p]
        src = hbm[f].at[pl.ds(at, n)] if f < 2 else fld.at[f, 1, pl.ds(1 + at, n)]
        k = d * 3 + p
        return remote(
            src, fld.at[f, 2 * d, pl.ds(1 + at, n)], ssem.at[f, k], rsem.at[f, k], dev(west if d else east, lat)
        )

    def ns(f, d, s):
        row = R if d else 1
        if s == 1 and f < 2:
            src = hbm[f].at[pl.ds(row - 1, 1)]
        else:
            src = fld.at[f, s, pl.ds(row, 1)]
        k = (6 if d else 9) + s
        return remote(
            src, fld.at[f, s, pl.ds(0 if d else R + 1, 1)], ssem.at[f, k], rsem.at[f, k],
            dev(lon, jnp.minimum(lat + 1, NLAT - 1) if d else jnp.maximum(lat - 1, 0)),
        )

    def north(fn):
        pl.when(lat > 0)(fn)

    def south(fn):
        pl.when(lat < NLAT - 1)(fn)

    def ns_start(f, s):
        north(lambda: ns(f, 0, s).start())
        south(lambda: ns(f, 1, s).start())

    def ns_recv(f, s):
        south(lambda: ns(f, 0, s).wait_recv())
        north(lambda: ns(f, 1, s).wait_recv())

    def ns_sent(f, s):
        north(lambda: ns(f, 0, s).wait_send())
        south(lambda: ns(f, 1, s).wait_send())

    def field_start(f):
        for p in range(3):
            for d in range(2):
                ew(f, d, p).start()
        ns_start(f, 1)

    def forward(f):
        for d in range(2):
            ew(f, d, 0).wait_recv()
            ew(f, d, 1).wait_recv()
            ns_start(f, 2 * d)

    def arrive(f, s):
        if s != 1:
            ew(f, s // 2, 2).wait_recv()
        ns_recv(f, s)

    def field_sent(f):
        for p in range(3):
            for d in range(2):
                ew(f, d, p).wait_send()
        for s in range(3):
            ns_sent(f, s)

    field_start(0)

    blank = jnp.zeros((W, C), BF)

    @pl.when(lat == 0)
    def _():
        for f in range(4):
            for s in range(3):
                fld[f, s, 0] = blank

    @pl.when(lat == NLAT - 1)
    def _():
        for f in range(4):
            for s in range(3):
                fld[f, s, R + 1] = blank

    field_start(1)

    for cp in wload:
        cp.wait()

    def turn(i, carry):
        wt2[i // 3, i % 3] = w2[i // 3, i % 3].T
        wt1[i // 3, i % 3] = w1[i // 3, i % 3].T
        return carry

    lax.fori_loop(0, TAPS, turn, 0)

    def conv_slot(f, s, weight, sign, fresh):
        b = sign * (s - 1) + 1
        taps = weight[:, b].reshape(3 * C, C)
        rows = R // 2

        def body(i, carry):
            left = jnp.concatenate(
                [
                    fld[f, s, pl.ds(1 + sign * a + rows * i, rows)].reshape(rows * W, C)
                    for a in (-1, 0, 1)
                ],
                axis=1,
            )
            part = jnp.dot(left, taps, preferred_element_type=F32).reshape(rows, W, C)
            if fresh:
                acc[pl.ds(rows * i, rows)] = part
            else:
                acc[pl.ds(rows * i, rows)] += part
            return carry

        lax.fori_loop(0, R // rows, body, 0)

    def oth_copy(f, s):
        return remote(fld.at[f, s], oth.at[s], osem.at[s], orem.at[s], dev(lon, sib))

    def oth2_copy(f):
        return remote(fld.at[f, 1, pl.ds(1, R)], oth2, o2s.at[0], o2r.at[0], dev(lon, sib))

    own[0].wait()
    forward(0)
    for i, s in enumerate((1, 0, 2)):
        arrive(0, s)

        @pl.when(core == 1)
        def _():
            oth_copy(0, s).start()

        conv_slot(0, s, w1, 1, i == 0)

    def gelu(i, carry):
        first = acc[i]
        cdf = 0.5 * (1.0 + lax.erf(first * np.float32(1 / np.sqrt(2.0))))
        fld[2, 1, 1 + i] = (first * cdf).astype(BF)
        dg[i] = cdf + first * (jnp.exp(-0.5 * first * first) * np.float32(1 / np.sqrt(2.0 * np.pi)))
        return carry

    lax.fori_loop(0, R, gelu, 0)
    field_start(2)

    @pl.when(core == 0)
    def _():
        oth2_copy(2).start()

    own[1].wait()
    forward(1)
    for i, s in enumerate((1, 0, 2)):
        arrive(1, s)

        @pl.when(core == 0)
        def _():
            oth_copy(1, s).start()

        conv_slot(1, s, wt2, -1, i == 0)

    def pre(i, carry):
        fld[3, 1, 1 + i] = (acc[i] * dg[i]).astype(BF)
        return carry

    lax.fori_loop(0, R, pre, 0)
    field_start(3)

    @pl.when(core == 1)
    def _():
        oth2_copy(3).start()

    forward(2)

    half = R * W
    ft[:, :half] = fld[3 - core, 1, pl.ds(1, R)].reshape(half, C).T
    oth2_copy(2).wait_recv()
    ft[:, half:] = oth2[...].reshape(half, C).T
    for s in range(3):
        oth_copy(0, s).wait_recv()
    sign = 1 - 2 * core

    def weight_terms(t, carry):
        slot, row = 1 + sign * (t % 3 - 1), 1 + sign * (t // 3 - 1)
        both = jnp.concatenate(
            [fld[core, slot, pl.ds(row, R)].reshape(half, C), oth[slot, pl.ds(row, R)].reshape(half, C)], axis=0
        )
        grad = jnp.dot(ft[...], both, preferred_element_type=F32)

        @pl.when(core == 0)
        def _():
            term[t] = grad.T.astype(BF).reshape(NY, 2, XC, C)

        @pl.when(core == 1)
        def _():
            term[t] = grad.astype(BF).reshape(NY, 2, XC, C)

        return carry

    lax.fori_loop(0, TAPS, weight_terms, 0)

    def first_ring(k, is_y):
        if is_y:
            device, yy = at_y(k)
            return remote(term.at[:, yy], r1a.at[k - 1], r1s.at[k - 1], r1r.at[k - 1], device)
        device, hh, ll = at_x(k)
        return remote(
            term.at[pl.ds(4 * hh, HALF), :, ll], r1b.at[k - 1], r1s.at[k - 1], r1r.at[k - 1], device
        )

    def second_ring(k, is_y):
        if is_y:
            device, yy = at_y(k)
            return remote(s1b.at[:, yy], r2.at[k - 1], r2s.at[k - 1], r2r.at[k - 1], device)
        device, hh, ll = at_x(k)
        return remote(s1a.at[pl.ds(4 * hh, HALF), ll], r2.at[k - 1], r2s.at[k - 1], r2r.at[k - 1], device)

    for c in (0, 1):

        @pl.when(core == c)
        def _():
            for k in (2, 1, 3):
                first_ring(k, c == 1).start()

    forward(3)

    def finish(f, base, weight, sgn, slot, hbm_out):
        for i, s in enumerate((1, 0, 2)):
            arrive(f, s)
            conv_slot(f, s, weight, sgn, i == 0)

        def body(i, carry):
            obuf[slot, i] = (fld[base, 1, 1 + i].astype(F32) + acc[i]).astype(BF)
            return carry

        lax.fori_loop(0, R, body, 0)
        cp = pltpu.make_async_copy(obuf.at[slot], hbm_out, lsem.at[4 + slot])
        cp.start()
        return cp

    outs = [finish(2, 0, w2, 1, 0, out_hbm), finish(3, 1, wt1, -1, 1, ig_hbm)]

    @pl.when(core == 1)
    def _():
        for k in (1, 2, 3):
            first_ring(k, True).wait_recv()

        def total(t, l):
            s = term[t, y, l].astype(F32)
            for k in range(3):
                s = s + r1a[k, t, l].astype(F32)
            return s

        def body(t, carry):
            for l in range(2):
                s1a[t, l] = total(t, l).astype(BF)
            return carry

        lax.fori_loop(0, TAPS, body, 0)
        for k in (2, 1, 3):
            second_ring(k, False).start()

        def mine(t, carry):
            u[t] = total(4 * xh + t, xl)
            return carry

        lax.fori_loop(0, HALF, mine, 0)

    @pl.when(core == 0)
    def _():
        for k in (1, 2, 3):
            first_ring(k, False).wait_recv()

        def total(t, yy):
            s = term[4 * xh + t, yy, xl].astype(F32)
            for k in range(3):
                s = s + r1b[k, t, yy].astype(F32)
            return s

        def body(t, carry):
            for yy in range(NY):
                s1b[t, yy] = total(t, yy).astype(BF)
            return carry

        lax.fori_loop(0, HALF, body, 0)
        for k in (2, 1, 3):
            second_ring(k, True).start()

        def mine(t, carry):
            u[t] = total(t, y)
            return carry

        lax.fori_loop(0, HALF, mine, 0)

    for k in (1, 2, 3):
        second_ring(k, True).wait_recv()

    summed = (u[...] + (r2[0].astype(F32) + r2[1].astype(F32) + r2[2].astype(F32))).astype(BF)
    zs[...] = (
        jnp.dot(pick_ref[...], summed.reshape(HALF * XC, C), preferred_element_type=F32).astype(BF).reshape(NZ, 32, C)
    )

    def z_copy(k):
        device, zz = at_z(k)
        return remote(zs.at[zz], r3.at[k - 1], r3s.at[k - 1], r3r.at[k - 1], device)

    for k in range(1, NZ):
        z_copy(k).start()
    q = zs[z].astype(F32)
    for k in range(1, NZ):
        z_copy(k).wait_recv()
        q = q + r3[k - 1].astype(F32)
    q = q * scale
    for l in range(NLAT):
        po[l, :, :YC] = q[:, l * YC : (l + 1) * YC]
        po[l, :, YC:] = jnp.zeros((32, 128 - YC), F32)

    def last_copy(k):
        to = (lat + k) % NLAT
        return remote(po.at[to], go.at[lat], r4s.at[k - 1], r4r.at[k - 1], dev(lon, to))

    for k in (1, 2, 3):
        last_copy(k).start()
    go[lat] = po[lat]
    for k in (1, 2, 3):
        last_copy(k).wait_recv()
    cp = pltpu.make_async_copy(go, g_hbm, lsem.at[6])
    cp.start()

    for f in range(4):
        field_sent(f)
    for s in range(3):
        oth_copy(0, s).wait_send()
    oth2_copy(2).wait_send()
    for c in (0, 1):

        @pl.when(core == c)
        def _():
            for k in (1, 2, 3):
                first_ring(k, c == 1).wait_send()
                second_ring(k, c == 0).wait_send()

    for k in range(1, NZ):
        z_copy(k).wait_send()
    for k in (1, 2, 3):
        last_copy(k).wait_send()
    for o in outs:
        o.wait()
    cp.wait()


def local(inputs, conv1_weight, conv2_weight, cotangent):
    scale = np.float32((R * NLAT * W * NLON) ** (-0.5))
    pick = jnp.asarray(selection(), BF)
    any_spec = pl.BlockSpec(memory_space=pl.ANY)
    vmem, dma = pltpu.VMEM, pltpu.SemaphoreType.DMA
    output, input_grad, g = pl.pallas_call(
        functools.partial(kernel, scale=scale),
        out_shape=[
            jax.ShapeDtypeStruct((R, W, C), BF),
            jax.ShapeDtypeStruct((R, W, C), BF),
            jax.ShapeDtypeStruct((NLAT, 32, 128), F32),
        ],
        in_specs=[any_spec] * 4 + [pl.BlockSpec(memory_space=pltpu.VMEM)],
        out_specs=[any_spec] * 3,
        scratch_shapes=[
            vmem((4, 3, R + 2, W, C), BF),
            vmem((3, 3, C, C), BF),
            vmem((3, 3, C, C), BF),
            vmem((3, 3, C, C), BF),
            vmem((3, 3, C, C), BF),
            vmem((R, W, C), F32),
            vmem((R, W, C), F32),
            vmem((2, R, W, C), BF),
            vmem((3, R + 2, W, C), BF),
            vmem((R, W, C), BF),
            vmem((C, 2 * R * W), BF),
            vmem((TAPS, NY, 2, XC, C), BF),
            vmem((3, TAPS, 2, XC, C), BF),
            vmem((3, HALF, NY, XC, C), BF),
            vmem((TAPS, 2, XC, C), BF),
            vmem((HALF, NY, XC, C), BF),
            vmem((3, HALF, XC, C), BF),
            vmem((HALF, XC, C), F32),
            vmem((NZ, 32, C), BF),
            vmem((NZ - 1, 32, C), BF),
            vmem((NLAT, 32, 128), F32),
            vmem((NLAT, 32, 128), F32),
            dma((4, 12)), dma((4, 12)),
            dma((3,)), dma((3,)),
            dma((1,)), dma((1,)),
            dma((3,)), dma((3,)),
            dma((3,)), dma((3,)),
            dma((NZ - 1,)), dma((NZ - 1,)),
            dma((3,)), dma((3,)),
            dma((7,)),
        ],
        compiler_params=pltpu.CompilerParams(
            collective_id=0, has_side_effects=True, vmem_limit_bytes=56 * 2**20
        ),
    )(inputs, cotangent, conv1_weight, conv2_weight, pick)
    rows = g[:, : HALF * ZC, :YC].reshape(NLAT, HALF, ZC, YC)
    grads = [
        jnp.concatenate([rows[c], rows[2 + c, 1:]], axis=0).reshape(3, 3, ZC, YC) for c in range(2)
    ]
    return (output, input_grad, *grads)


def solution(mesh):
    in_specs = (P("lat", "lon", None), P(), P(), P("lat", "lon", None))
    out_specs = (
        P("lat", "lon", None),
        P("lat", "lon", None),
        P(None, None, "lon", "lat"),
        P(None, None, "lon", "lat"),
    )
    return jax.shard_map(local, mesh=mesh, in_specs=in_specs, out_specs=out_specs, check_vma=False)
```

```python
import functools

import jax
import jax.numpy as jnp
import numpy as np
from jax import lax
from jax.experimental import pallas as pl
from jax.experimental.pallas import tpu as pltpu
from jax.sharding import PartitionSpec as P

MESH = pl.DeviceIdType.MESH
BF = jnp.bfloat16
F32 = jnp.float32

NY, NX, NZ = 4, 4, 8
NLON, NLAT, NCOL = 64, 4, 8
R, W, C = 8, 64, 384
G = W // NZ
TAPS, HALF = 9, 5
YC, XC, ZC = 96, 48, 6


def selection():
    pick = np.zeros((NZ * 32, HALF * XC), np.float32)
    for z in range(NZ):
        for t in range(HALF):
            for r in range(ZC):
                pick[z * 32 + t * ZC + r, t * XC + z * ZC + r] = 1.0
    return pick


def kernel(
    x_hbm, c_hbm, w1_hbm, w2_hbm, pick_ref,
    out_hbm, ig_hbm, g_hbm,
    fld, w1, w2, wt1, wt2, acc, dg, obuf, oth, oth2, ft, term,
    r1a, r1b, s1a, s1b, r2, u, zs, r3, po, go,
    asem, arem, hsem, hrem, osem, orem, o2s, o2r, r1s, r1r, r2s, r2r, r3s, r3r, r4s, r4r, lsem,
    *, scale,
):
    lon, lat = lax.axis_index("lon"), lax.axis_index("lat")
    y, xl, z = lon // 16, (lon // 8) % 2, lon % 8
    xh, core = lat // 2, lat % 2
    x = xh * 2 + xl
    col = lon // NZ
    east, west = (col + 1) % NCOL, (col + NCOL - 1) % NCOL
    sib = xh * 2 + 1 - core

    def dev(o, a):
        return {"lon": o, "lat": a}

    def at_y(k):
        return dev((((y + k) % NY) * 2 + xl) * NZ + z, lat), (y + k) % NY

    def at_x(k):
        xx = (x + k) % NX
        return dev((y * 2 + xx % 2) * NZ + z, (xx // 2) * 2 + core), xx // 2, xx % 2

    def at_z(k):
        zz = (z + k) % NZ
        return dev((y * 2 + xl) * NZ + zz, lat), zz

    def cols(zz):
        return pl.ds(pl.multiple_of(zz * G, G), G)

    hbm = (x_hbm, c_hbm)
    own = [
        pltpu.make_async_copy(hbm[f].at[:, cols(z)], fld.at[f, 1, pl.ds(1, R), cols(z)], lsem.at[f]) for f in range(2)
    ]
    wload = [pltpu.make_async_copy(s, d, lsem.at[2 + i]) for i, (s, d) in enumerate(((w1_hbm, w1), (w2_hbm, w2)))]
    for cp in own + wload:
        cp.start()

    barrier = pltpu.get_barrier_semaphore()
    peers = [dev(o * NZ + z, (lat + k) % NLAT) for o in (east, west) for k in (0, 1, 3)]
    peers += [dev(lon, (lat + k) % NLAT) for k in (1, 2, 3)]
    peers += [at_y(k)[0] for k in (1, 2, 3)] + [at_x(k)[0] for k in (1, 2, 3)] + [at_z(k)[0] for k in range(1, NZ)]
    for peer in peers:
        pl.semaphore_signal(barrier, inc=1, device_id=peer, device_id_type=MESH)
    pl.semaphore_wait(barrier, len(peers))

    def remote(src, dst, s, r, device):
        return pltpu.make_async_remote_copy(
            src_ref=src, dst_ref=dst, send_sem=s, recv_sem=r, device_id=device, device_id_type=MESH
        )

    order = (4, 3, 5, 2, 6, 1, 7)

    def gather(f, k):
        device, zz = at_z(k)
        return remote(
            hbm[f].at[:, cols(zz)], fld.at[f, 1, pl.ds(1, R), cols(z)], asem.at[f, k - 1], arem.at[f, k - 1], device
        )

    def give_back(f, k):
        device, zz = at_z(k)
        out = (out_hbm, ig_hbm)[f]
        return remote(
            obuf.at[f, :, cols(zz)], out.at[:, cols(z)], asem.at[2 + f, k - 1], arem.at[2 + f, k - 1], device
        )

    def halo(f, sx, sy):
        rows_from, rows_to = {0: ((1, R), 1), -1: ((1, 1), R + 1), 1: ((R, 1), 0)}[sy]
        src_cols, slot, dst_cols = {
            0: (pl.ds(0, W), 1, pl.ds(0, W)),
            1: (pl.ds(W - G, G), 0, pl.ds(0, G)),
            -1: (pl.ds(0, G), 2, pl.ds(W - G, G)),
        }[sx]
        n = rows_from[1]
        k = (sx + 1) * 3 + sy + 1
        to_lat = jnp.clip(lat + sy, 0, NLAT - 1)
        return remote(
            fld.at[f, 1, pl.ds(rows_from[0], n), src_cols], fld.at[f, slot, pl.ds(rows_to, n), dst_cols],
            hsem.at[f, k], hrem.at[f, k], dev({0: col, 1: east, -1: west}[sx] * NZ + z, to_lat),
        )

    def guarded(sy, fn, incoming):
        if sy == 0:
            fn()
        elif (sy < 0) != incoming:
            pl.when(lat > 0)(fn)
        else:
            pl.when(lat < NLAT - 1)(fn)

    sides = [(0, -1), (0, 1), (1, 0), (-1, 0), (1, -1), (1, 1), (-1, -1), (-1, 1)]

    def halo_start(f):
        for sx, sy in sides:
            guarded(sy, halo(f, sx, sy).start, False)

    def halo_sent(f):
        for sx, sy in sides:
            guarded(sy, halo(f, sx, sy).wait_send, False)

    def shift(f, rows):
        for i in rows:
            fld[f, 0, i, G:] = fld[f, 1, i, : W - G]
            fld[f, 2, i, : W - G] = fld[f, 1, i, G:]

    def arrive(f, s):
        sx = 1 - s
        for sy in (0, -1, 1):
            if sx or sy:
                guarded(sy, halo(f, sx, sy).wait_recv, True)
        if s == 1:
            shift(f, (0, R + 1))

    def gathered(f):
        for k in order:
            if f or k not in (1, 7):
                gather(f, k).wait_recv()
        own[f].wait()
        halo_start(f)
        shift(f, range(1, R + 1))

    for k in order:
        gather(0, k).start()

    blank = jnp.zeros((W, C), BF)

    @pl.when(lat == 0)
    def _():
        for f in range(4):
            for s in range(3):
                fld[f, s, 0] = blank

    @pl.when(lat == NLAT - 1)
    def _():
        for f in range(4):
            for s in range(3):
                fld[f, s, R + 1] = blank

    for cp in wload:
        cp.wait()

    def turn(i, carry):
        wt2[i // 3, i % 3] = w2[i // 3, i % 3].T
        wt1[i // 3, i % 3] = w1[i // 3, i % 3].T
        return carry

    lax.fori_loop(0, TAPS, turn, 0)

    def conv_slot(f, s, weight, sign, fresh):
        b = sign * (s - 1) + 1
        taps = weight[:, b].reshape(3 * C, C)
        left = jnp.concatenate(
            [fld[f, s, pl.ds(1 + sign * a, R)].reshape(R * W, C) for a in (-1, 0, 1)], axis=1
        )
        part = jnp.dot(left, taps, preferred_element_type=F32).reshape(R, W, C)
        if fresh:
            acc[...] = part
        else:
            acc[...] += part

    def oth_copy(f, s):
        return remote(fld.at[f, s], oth.at[s], osem.at[s], orem.at[s], dev(lon, sib))

    def oth2_copy(f):
        return remote(fld.at[f, 1, pl.ds(1, R)], oth2, o2s.at[0], o2r.at[0], dev(lon, sib))

    for k in (1, 7):
        gather(0, k).wait_recv()
    for k in order:
        gather(1, k).start()
    gathered(0)
    for i, s in enumerate((1, 0, 2)):
        arrive(0, s)

        @pl.when(core == 1)
        def _():
            oth_copy(0, s).start()

        conv_slot(0, s, w1, 1, i == 0)

    def gelu(i, carry):
        first = acc[i]
        cdf = 0.5 * (1.0 + lax.erf(first * np.float32(1 / np.sqrt(2.0))))
        fld[2, 1, 1 + i] = (first * cdf).astype(BF)
        dg[i] = cdf + first * (jnp.exp(-0.5 * first * first) * np.float32(1 / np.sqrt(2.0 * np.pi)))
        return carry

    lax.fori_loop(0, R, gelu, 0)
    halo_start(2)

    @pl.when(core == 0)
    def _():
        oth2_copy(2).start()

    shift(2, range(1, R + 1))
    gathered(1)

    def finish(f, base, weight, sgn, slot, hbm_out):
        for i, s in enumerate((1, 0, 2)):
            arrive(f, s)
            conv_slot(f, s, weight, sgn, i == 0)

        def body(i, carry):
            obuf[slot, i] = (fld[base, 1, 1 + i].astype(F32) + acc[i]).astype(BF)
            return carry

        lax.fori_loop(0, R, body, 0)
        for k in order:
            give_back(slot, k).start()
        cp = pltpu.make_async_copy(obuf.at[slot, :, cols(z)], hbm_out.at[:, cols(z)], lsem.at[4 + slot])
        cp.start()
        return cp

    outs = [finish(2, 0, w2, 1, 0, out_hbm)]

    for i, s in enumerate((1, 0, 2)):
        arrive(1, s)

        @pl.when(core == 0)
        def _():
            oth_copy(1, s).start()

        conv_slot(1, s, wt2, -1, i == 0)

    def pre(i, carry):
        fld[3, 1, 1 + i] = (acc[i] * dg[i]).astype(BF)
        return carry

    lax.fori_loop(0, R, pre, 0)
    halo_start(3)

    @pl.when(core == 1)
    def _():
        oth2_copy(3).start()

    half = R * W
    ft[:, :half] = fld[3 - core, 1, pl.ds(1, R)].reshape(half, C).T
    oth2_copy(2).wait_recv()
    ft[:, half:] = oth2[...].reshape(half, C).T
    for s in range(3):
        oth_copy(0, s).wait_recv()
    sign = 1 - 2 * core

    def weight_terms(t):
        slot, row = 1 + sign * ((t // 3 + 1) % 3 - 1), 1 + sign * (t % 3 - 1)
        both = jnp.concatenate(
            [fld[core, slot, pl.ds(row, R)].reshape(half, C), oth[slot, pl.ds(row, R)].reshape(half, C)], axis=0
        )
        grad = jnp.dot(ft[...], both, preferred_element_type=F32)

        @pl.when(core == 0)
        def _():
            term[t] = grad.T.astype(BF).reshape(NY, 2, XC, C)

        @pl.when(core == 1)
        def _():
            term[t] = grad.astype(BF).reshape(NY, 2, XC, C)

    def tap_of(p, hh):
        return jnp.minimum(2 * p + hh, TAPS - 1)

    def first_ring(p, k, is_y, n):
        sems = r1s.at[p, k - 1], r1r.at[p, k - 1]
        if is_y:
            device, yy = at_y(k)
            at = pl.ds(2 * p, n)
            return remote(term.at[at, yy], r1a.at[k - 1, at], *sems, device)
        device, hh, ll = at_x(k)
        return remote(term.at[tap_of(p, hh), :, ll], r1b.at[k - 1, p], *sems, device)

    def second_ring(p, k, is_y):
        sems = r2s.at[p, k - 1], r2r.at[p, k - 1]
        if is_y:
            device, yy = at_y(k)
            return remote(s1b.at[p, yy], r2.at[k - 1, p], *sems, device)
        device, hh, ll = at_x(k)
        return remote(s1a.at[tap_of(p, hh), ll], r2.at[k - 1, p], *sems, device)

    def piece(p, n):
        def body(i, carry):
            weight_terms(2 * p + i)
            return carry

        lax.fori_loop(0, n, body, 0)
        for c in (0, 1):

            @pl.when(core == c)
            def _():
                for k in (2, 1, 3):
                    first_ring(p, k, c == 1, n).start()

    def pieces(lo, hi):
        def body(p, carry):
            piece(p, 2)
            return carry

        lax.fori_loop(lo, hi, body, 0)

    pieces(0, 3)
    shift(3, range(1, R + 1))
    outs += [finish(3, 1, wt1, -1, 1, ig_hbm)]
    pieces(3, 4)
    piece(4, 1)

    def sum_y(p, n):
        for k in (1, 2, 3):
            first_ring(p, k, True, n).wait_recv()

        def total(t, l):
            v = term[t, y, l].astype(F32)
            for k in range(3):
                v = v + r1a[k, t, l].astype(F32)
            return v

        for i in range(n):
            for l in range(2):
                s1a[2 * p + i, l] = total(2 * p + i, l).astype(BF)
        for k in (2, 1, 3):
            second_ring(p, k, False).start()
        u[p] = total(tap_of(p, xh), xl)

    def sum_x(p, n):
        for k in (1, 2, 3):
            first_ring(p, k, False, n).wait_recv()

        def total(yy):
            v = term[tap_of(p, xh), yy, xl].astype(F32)
            for k in range(3):
                v = v + r1b[k, p, yy].astype(F32)
            return v

        for yy in range(NY):
            s1b[p, yy] = total(yy).astype(BF)
        for k in (2, 1, 3):
            second_ring(p, k, True).start()
        u[p] = total(y)

    def sums(lo, hi, n):
        for c in (0, 1):

            @pl.when(core == c)
            def _():
                def body(p, carry):
                    (sum_y if c else sum_x)(p, n)
                    return carry

                lax.fori_loop(lo, hi, body, 0)

    sums(0, 4, 2)
    sums(4, 5, 1)
    for p in range(HALF):
        for k in (1, 2, 3):
            second_ring(p, k, True).wait_recv()

    summed = (u[...] + (r2[0].astype(F32) + r2[1].astype(F32) + r2[2].astype(F32))).astype(BF)
    zs[...] = (
        jnp.dot(pick_ref[...], summed.reshape(HALF * XC, C), preferred_element_type=F32).astype(BF).reshape(NZ, 32, C)
    )

    def z_copy(k):
        device, zz = at_z(k)
        return remote(zs.at[zz], r3.at[k - 1], r3s.at[k - 1], r3r.at[k - 1], device)

    for k in range(1, NZ):
        z_copy(k).start()
    q = zs[z].astype(F32)
    for k in range(1, NZ):
        z_copy(k).wait_recv()
        q = q + r3[k - 1].astype(F32)
    q = q * scale
    for l in range(NLAT):
        po[l, :, :YC] = q[:, l * YC : (l + 1) * YC]
        po[l, :, YC:] = jnp.zeros((32, 128 - YC), F32)

    def last_copy(k):
        to = (lat + k) % NLAT
        return remote(po.at[to], go.at[lat], r4s.at[k - 1], r4r.at[k - 1], dev(lon, to))

    for k in (1, 2, 3):
        last_copy(k).start()
    go[lat] = po[lat]
    for k in (1, 2, 3):
        last_copy(k).wait_recv()
    cp = pltpu.make_async_copy(go, g_hbm, lsem.at[6])
    cp.start()

    for f in range(4):
        halo_sent(f)
    for f in range(2):
        for k in order:
            gather(f, k).wait_send()
            give_back(f, k).wait_send()
            give_back(f, k).wait_recv()
    for s in range(3):
        oth_copy(0, s).wait_send()
    oth2_copy(2).wait_send()
    for c in (0, 1):

        @pl.when(core == c)
        def _():
            for p in range(HALF):
                for k in (1, 2, 3):
                    first_ring(p, k, c == 1, 2 if p < 4 else 1).wait_send()
                    second_ring(p, k, c == 0).wait_send()

    for k in range(1, NZ):
        z_copy(k).wait_send()
    for k in (1, 2, 3):
        last_copy(k).wait_send()
    for o in outs:
        o.wait()
    cp.wait()


def place(o_ref, i_ref, g_ref, out_ref, ig_ref, g1_ref, g2_ref, sem):
    copies = [
        pltpu.make_async_copy(s, d, sem.at[i]) for i, (s, d) in enumerate(((o_ref, out_ref), (i_ref, ig_ref)))
    ]
    for cp in copies:
        cp.start()
    for t in range(TAPS):
        a, b = t % 3, (t // 3 + 1) % 3
        p, hh = t // 2, t % 2
        for c, ref in enumerate((g1_ref, g2_ref)):
            ref[a, b] = g_ref[2 * hh + c, p * ZC : (p + 1) * ZC, :YC]
    for cp in copies:
        cp.wait()


def local(inputs, conv1_weight, conv2_weight, cotangent):
    scale = np.float32((R * NLAT * W * NLON) ** (-0.5))
    pick = jnp.asarray(selection(), BF)
    any_spec = pl.BlockSpec(memory_space=pl.ANY)
    vmem, dma = pltpu.VMEM, pltpu.SemaphoreType.DMA
    output, input_grad, g = pl.pallas_call(
        functools.partial(kernel, scale=scale),
        out_shape=[
            jax.ShapeDtypeStruct((R, W, C), BF),
            jax.ShapeDtypeStruct((R, W, C), BF),
            jax.ShapeDtypeStruct((NLAT, 32, 128), F32),
        ],
        in_specs=[any_spec] * 4 + [pl.BlockSpec(memory_space=pltpu.VMEM)],
        out_specs=[any_spec] * 3,
        scratch_shapes=[
            vmem((4, 3, R + 2, W, C), BF),
            vmem((3, 3, C, C), BF),
            vmem((3, 3, C, C), BF),
            vmem((3, 3, C, C), BF),
            vmem((3, 3, C, C), BF),
            vmem((R, W, C), F32),
            vmem((R, W, C), F32),
            vmem((2, R, W, C), BF),
            vmem((3, R + 2, W, C), BF),
            vmem((R, W, C), BF),
            vmem((C, 2 * R * W), BF),
            vmem((TAPS, NY, 2, XC, C), BF),
            vmem((3, TAPS, 2, XC, C), BF),
            vmem((3, HALF, NY, XC, C), BF),
            vmem((TAPS, 2, XC, C), BF),
            vmem((HALF, NY, XC, C), BF),
            vmem((3, HALF, XC, C), BF),
            vmem((HALF, XC, C), F32),
            vmem((NZ, 32, C), BF),
            vmem((NZ - 1, 32, C), BF),
            vmem((NLAT, 32, 128), F32),
            vmem((NLAT, 32, 128), F32),
            dma((4, 7)), dma((4, 7)),
            dma((4, 9)), dma((4, 9)),
            dma((3,)), dma((3,)),
            dma((1,)), dma((1,)),
            dma((HALF, 3)), dma((HALF, 3)),
            dma((HALF, 3)), dma((HALF, 3)),
            dma((NZ - 1,)), dma((NZ - 1,)),
            dma((3,)), dma((3,)),
            dma((7,)),
        ],
        compiler_params=pltpu.CompilerParams(
            collective_id=0, has_side_effects=True, vmem_limit_bytes=56 * 2**20
        ),
    )(inputs, cotangent, conv1_weight, conv2_weight, pick)
    return pl.pallas_call(
        place,
        out_shape=[
            jax.ShapeDtypeStruct((R, W, C), BF),
            jax.ShapeDtypeStruct((R, W, C), BF),
            jax.ShapeDtypeStruct((3, 3, ZC, YC), F32),
            jax.ShapeDtypeStruct((3, 3, ZC, YC), F32),
        ],
        in_specs=[pl.BlockSpec(memory_space=pltpu.VMEM)] * 3,
        out_specs=[any_spec] * 2 + [pl.BlockSpec(memory_space=pltpu.VMEM)] * 2,
        scratch_shapes=[dma((2,))],
    )(output, input_grad, g)


def solution(mesh):
    in_specs = (P("lat", "lon", None), P(), P(), P("lat", "lon", None))
    out_specs = (
        P("lat", "lon", None),
        P("lat", "lon", None),
        P(None, None, "lon", "lat"),
        P(None, None, "lon", "lat"),
    )
    return jax.shard_map(local, mesh=mesh, in_specs=in_specs, out_specs=out_specs, check_vma=False)
```
